32 devices in a mesh: batch: 8 (over z, core), seq: 2 (over y), head: 2 (over x).
Axes of the slice: x: 2, y: 2, z: 4, core: 2. Of those that a mesh axis runs over, the one named last changes fastest.
Arguments:
- tokens: float32 [8, 256, 768], P('batch', 'seq'), may hold values from -6 to 6
- cotangent: float32 [8, 256, 768], P('batch', 'seq'), may hold values from -6 to 6
- norm_gain: float32 [2, 768], replicated, may hold values from 0.1 to 1.9
- weight_zx: bfloat16 [2, 768, 2, 1536], P(None, None, None, 'head'), may hold values from -0.21875 to 0.21875
- weight_bc: bfloat16 [2, 768, 256], P(None, None, 'head'), may hold values from -0.21875 to 0.21875
- weight_step: bfloat16 [2, 768, 24], P(None, None, 'head'), may hold values from -0.21875 to 0.21875
- step_bias: float32 [2, 24], P(None, 'head'), may hold values from -6 to -2
- log_rate: float32 [2, 24], P(None, 'head'), may hold values from -3 to 2
- skip_gain: float32 [2, 24], P(None, 'head'), may hold values from 0.5 to 2
- taps_x: float32 [2, 4, 1536], P(None, None, 'head'), may hold values from -3 to 3
- offset_x: float32 [2, 1536], P(None, 'head'), may hold values from -3 to 3
- taps_bc: float32 [2, 4, 256], P(None, None, 'head'), may hold values from -3 to 3
- offset_bc: float32 [2, 256], P(None, 'head'), may hold values from -3 to 3
- gate_gain: float32 [2, 1536], P(None, 'head'), may hold values from 0.1 to 1.9
- weight_out: bfloat16 [2, 1536, 768], P(None, 'head'), may hold values from -0.15625 to 0.15625
Outputs:
- output: float32 [8, 256, 768], P('batch', 'seq')
- grad_tokens: float32 [8, 256, 768], P('batch', 'seq')
- grad_norm_gain: float32 [2, 768], replicated
- grad_weight_zx: float32 [2, 768, 2, 1536], P(None, ('batch', 'seq'), None, 'head')
- grad_weight_bc: float32 [2, 768, 256], P(None, ('batch', 'seq'), 'head')
- grad_weight_step: float32 [2, 768, 24], P(None, ('batch', 'seq'), 'head')
- grad_step_bias: float32 [2, 24], P(None, 'head')
- grad_log_rate: float32 [2, 24], P(None, 'head')
- grad_skip_gain: float32 [2, 24], P(None, 'head')
- grad_taps_x: float32 [2, 4, 1536], P(None, None, 'head')
- grad_offset_x: float32 [2, 1536], P(None, 'head')
- grad_taps_bc: float32 [2, 4, 256], P(None, None, 'head')
- grad_offset_bc: float32 [2, 256], P(None, 'head')
- grad_gate_gain: float32 [2, 1536], P(None, 'head')
- grad_weight_out: float32 [2, 1536, 768], P(None, 'head', ('batch', 'seq'))
The draws below stay inside these ranges and needn't reach their ends.
All inputs are finite; a program needn't handle non-finite values.
Results may differ from the reference program's by a relative error of at most 0.024.
Values may be sent and summed in bfloat16 or wider, within the bound.
No kernel may reach another device: no remote copies, remote signals or barrier semaphores. Data moves between devices by JAX's collectives and lax.ppermute only.
A program may use at most 128 MiB of HBM per device.

```python
import jax
import jax.numpy as jnp
from jax import lax

D = 768
INNER = 1536
STATE = 128
HEADDIM = 64
CONV = 4
GROUP = 128
LAYERS = 2
HEADS = 24
SEQS = 8
LEN = 256


def levels(rng, dims, cuts, smallest, high):
    def one(position, blocks):
        steps = jax.random.uniform(jax.random.fold_in(jax.random.fold_in(rng, 6), position), (blocks,), jnp.float32, smallest / len(cuts), high / len(cuts))
        return jnp.repeat(jnp.exp(steps), dims[position] // blocks).reshape((-1,) + (1,) * (len(dims) - position - 1))

    loudness = one(*cuts[0])
    for cut in cuts[1:]:
        loudness = loudness * one(*cut)
    return loudness


def bell_draw(stream_key, extent, scale, reach, shards=(), held_as=jnp.bfloat16):
    entries = jax.random.normal(stream_key, extent, jnp.float32) * scale
    if len(shards) > 0:
        entries = levels(stream_key, extent, shards, -0.22, 0.18) * entries
    return jnp.clip(entries, min=-reach, max=reach).astype(held_as)


def setup_inputs(seed: int = 0) -> dict:
    key_of = jax.random.split(jax.random.key(seed), 16)
    tokens = bell_draw(key_of[0], (SEQS, LEN, D), 1.0, 6.0, ((0, 8), (1, 2)), jnp.float32)
    cotangent = bell_draw(key_of[1], (SEQS, LEN, D), 1.0, 6.0, ((0, 8), (1, 2)), jnp.float32)
    norm_gain = jnp.clip(1.0 + 0.18 * jax.random.normal(key_of[2], (LAYERS, D), jnp.float32), 0.1, 1.9)
    weight_zx = bell_draw(key_of[3], (LAYERS, D, 2, INNER), D ** -0.5, 0.21875, ((3, 2),))
    weight_bc = bell_draw(key_of[4], (LAYERS, D, 2 * STATE), D ** -0.5, 0.21875, ((2, 2),))
    weight_step = bell_draw(key_of[5], (LAYERS, D, HEADS), D ** -0.5, 0.21875, ((2, 2),))
    step_bias = jnp.clip(-6.0 + 4.0 * jax.random.uniform(key_of[6], (LAYERS, HEADS), jnp.float32) ** levels(key_of[6], (LAYERS, HEADS), ((1, 2),), -0.2, 0.2), -6.0, -2.0)
    log_rate = jnp.clip(-3.0 + 5.0 * jax.random.uniform(key_of[7], (LAYERS, HEADS), jnp.float32) ** levels(key_of[7], (LAYERS, HEADS), ((1, 2),), -0.2, 0.2), -3.0, 2.0)
    skip_gain = jnp.clip(0.5 + 1.5 * jax.random.uniform(key_of[8], (LAYERS, HEADS), jnp.float32) ** levels(key_of[8], (LAYERS, HEADS), ((1, 2),), -0.2, 0.2), 0.5, 2.0)
    taps_x = bell_draw(key_of[9], (LAYERS, CONV, INNER), CONV ** -0.5, 3.0, ((2, 2),), jnp.float32)
    offset_x = bell_draw(key_of[10], (LAYERS, INNER), 0.5, 3.0, ((1, 2),), jnp.float32)
    taps_bc = bell_draw(key_of[11], (LAYERS, CONV, 2 * STATE), CONV ** -0.5, 3.0, ((2, 2),), jnp.float32)
    offset_bc = bell_draw(key_of[12], (LAYERS, 2 * STATE), 0.5, 3.0, ((1, 2),), jnp.float32)
    gate_gain = jnp.clip(1.0 + 0.18 * jax.random.normal(key_of[13], (LAYERS, INNER), jnp.float32), 0.1, 1.9)
    weight_out = bell_draw(key_of[14], (LAYERS, INNER, D), INNER ** -0.5, 0.15625, ((1, 2),))
    return dict(tokens=tokens, cotangent=cotangent, norm_gain=norm_gain, weight_zx=weight_zx, weight_bc=weight_bc, weight_step=weight_step, step_bias=step_bias, log_rate=log_rate, skip_gain=skip_gain, taps_x=taps_x, offset_x=offset_x, taps_bc=taps_bc, offset_bc=offset_bc, gate_gain=gate_gain, weight_out=weight_out)


epsilon = 1e-05

def mixing(form, left, right):
    return jnp.einsum(form, left.astype(jnp.float32), right.astype(jnp.float32))

def silu_of(value):
    return value * jax.nn.sigmoid(value)

def lead_axes(value):
    return tuple(range(value.ndim - 1))

def norm_forward(stream, gain):
    inv_rms = lax.rsqrt(lax.optimization_barrier(jnp.mean(stream * stream, axis=-1, keepdims=True)) + epsilon)
    normed = (stream * inv_rms * gain).astype(jnp.bfloat16)
    return (normed, inv_rms)

def norm_back(grad, d_normed, stream, inv_rms, gain):
    scaled = d_normed * gain
    d_gain = lax.optimization_barrier(jnp.sum(d_normed * stream * inv_rms, axis=lead_axes(stream)))
    grad_in = grad + inv_rms * scaled - stream * inv_rms ** 3 * lax.optimization_barrier(jnp.mean(scaled * stream, axis=-1, keepdims=True))
    return (grad_in, d_gain)

def project_in(normed, weight_zx, weight_bc, weight_step):
    width = weight_zx.shape[0]
    proj_zx = jnp.dot(normed, weight_zx.reshape(width, -1), preferred_element_type=jnp.float32).astype(jnp.bfloat16)
    pre_bc = jnp.dot(normed, weight_bc, preferred_element_type=jnp.float32).astype(jnp.bfloat16)
    step_raw = jnp.dot(normed, weight_step, preferred_element_type=jnp.float32)
    return (proj_zx, pre_bc, step_raw)

def conv_forward(padded, taps, offset):
    kernel = taps.shape[0]
    length = padded.shape[0] - kernel + 1
    values = padded.astype(jnp.float32)
    total = offset + taps[0] * values[0:length]
    for index in range(1, kernel):
        total = total + taps[index] * values[index:index + length]
    return total

def conv_backward(d_out, padded, taps, offset):
    kernel = taps.shape[0]
    length = padded.shape[0] - kernel + 1
    values = padded.astype(jnp.float32)
    before = conv_forward(padded, taps, offset)
    sigma = jax.nn.sigmoid(before)
    d_pre = d_out * sigma * (1.0 + before * (1.0 - sigma))
    d_taps = jnp.stack([lax.optimization_barrier(jnp.sum(d_pre * values[index:index + length], axis=0)) for index in range(kernel)])
    d_offset = lax.optimization_barrier(jnp.sum(d_pre, axis=0))
    d_pad = jnp.pad(taps[0] * d_pre, ((0, kernel - 1), (0, 0)))
    for index in range(1, kernel):
        d_pad = d_pad + jnp.pad(taps[index] * d_pre, ((index, kernel - 1 - index), (0, 0)))
    return (d_pad, d_taps, d_offset)

def decay_parts(step_raw, step_bias, log_rate):
    step_size = jax.nn.softplus(step_raw + step_bias)
    rate = -jnp.exp(log_rate)
    cumul = jnp.cumsum(step_size * rate, axis=-2)
    return (step_size, cumul)

def pair_decay(cumul):
    length = cumul.shape[0]
    rows = lax.broadcasted_iota(jnp.int32, (length, length), 0)
    cols = lax.broadcasted_iota(jnp.int32, (length, length), 1)
    lower = (rows >= cols)[None]
    spread = cumul.T[:, :, None] - cumul.T[:, None, :]
    return jnp.where(lower, jnp.exp(jnp.where(lower, spread, 0.0)), 0.0)

def ssd_group(conv_x, full_bc, step_size, cumul):
    length, heads = step_size.shape
    state = full_bc.shape[1] // 2
    b_mat = full_bc[:, :state]
    c_mat = full_bc[:, state:]
    xheads = conv_x.reshape(length, heads, -1)
    gram = jnp.dot(c_mat, b_mat.T, preferred_element_type=jnp.float32)
    decay = pair_decay(cumul)
    weights_mat = (gram[None] * decay * step_size.T[:, None, :]).astype(jnp.bfloat16)
    intra = mixing('hts,shp->thp', weights_mat, xheads)
    tail = jnp.exp(cumul[-1][None, :] - cumul)
    scaled_x = (xheads.astype(jnp.float32) * (step_size * tail)[:, :, None]).astype(jnp.bfloat16)
    end_state = mixing('shp,sn->hpn', scaled_x, b_mat)
    return (intra, end_state)

def ssd_output(intra, state_in, conv_x, full_bc, cumul, skip):
    length, heads = cumul.shape
    state = full_bc.shape[1] // 2
    c_mat = full_bc[:, state:]
    xheads = conv_x.reshape(length, heads, -1).astype(jnp.float32)
    carried = mixing('tn,hpn->thp', c_mat, state_in.astype(jnp.bfloat16))
    mixed = intra + jnp.exp(cumul)[:, :, None] * carried + skip[None, :, None] * xheads
    return (mixed.reshape(length, -1), carried)

def gate_local(mixed, proj_zx):
    inner_local = mixed.shape[-1]
    zpart = proj_zx[..., :inner_local].astype(jnp.float32)
    gated = mixed * silu_of(zpart)
    return (gated, lax.optimization_barrier(jnp.sum(gated * gated, axis=-1)))

def gate_apply(gated, squares, gain, inner):
    inv_gate = lax.rsqrt(squares / inner + epsilon)[..., None]
    return ((gated * inv_gate * gain).astype(jnp.bfloat16), inv_gate)

def gate_back(scaled, gated, inv_gate, dots, inner):
    return inv_gate * scaled - gated * inv_gate ** 3 * dots[..., None] / inner

def gate_inputs(d_gated, mixed, proj_zx):
    inner_local = mixed.shape[-1]
    zpart = proj_zx[..., :inner_local].astype(jnp.float32)
    sigma = jax.nn.sigmoid(zpart)
    d_mixed = d_gated * zpart * sigma
    d_zpart = d_gated * mixed * sigma * (1.0 + zpart * (1.0 - sigma))
    return (d_mixed, d_zpart)

def ssd_back_carried(d_mixed, conv_x, full_bc, cumul, carried, state_in, skip):
    length, heads = cumul.shape
    state = full_bc.shape[1] // 2
    c_mat = full_bc[:, state:]
    d_heads = d_mixed.reshape(length, heads, -1)
    xheads = conv_x.reshape(length, heads, -1).astype(jnp.float32)
    d_skip = lax.optimization_barrier(jnp.sum(d_heads * xheads, axis=(0, 2)))
    d_x = skip[None, :, None] * d_heads
    expo = jnp.exp(cumul)
    d_cumul = lax.optimization_barrier(jnp.sum(d_heads * carried, axis=2)) * expo
    d_scaled = (d_heads * expo[:, :, None]).astype(jnp.bfloat16)
    d_cmat = mixing('thp,hpn->tn', d_scaled, state_in.astype(jnp.bfloat16))
    d_state = mixing('thp,tn->hpn', d_scaled, c_mat)
    return (d_x, d_cumul, d_cmat, d_state, d_skip)

def ssd_back_rest(d_mixed, d_x, d_cumul, d_cmat, later_grad, state_in, conv_x, full_bc, step_raw, step_size, cumul, step_bias, log_rate):
    length, heads = cumul.shape
    state = full_bc.shape[1] // 2
    b_mat = full_bc[:, :state]
    c_mat = full_bc[:, state:]
    xheads_b = conv_x.reshape(length, heads, -1)
    xheads = xheads_b.astype(jnp.float32)
    d_heads = d_mixed.reshape(length, heads, -1)
    last = cumul[-1]
    d_last = jnp.exp(last) * lax.optimization_barrier(jnp.sum(later_grad * state_in, axis=(1, 2)))
    later_b = later_grad.astype(jnp.bfloat16)
    tail = jnp.exp(last[None, :] - cumul)
    factor = step_size * tail
    scaled_x = (xheads * factor[:, :, None]).astype(jnp.bfloat16)
    d_scaled_x = mixing('hpn,sn->shp', later_b, b_mat)
    d_bmat = mixing('shp,hpn->sn', scaled_x, later_b)
    d_x = d_x + d_scaled_x * factor[:, :, None]
    d_factor = lax.optimization_barrier(jnp.sum(d_scaled_x * xheads, axis=2))
    d_step = d_factor * tail
    moved = d_factor * factor
    d_cumul = d_cumul - moved
    d_last = d_last + lax.optimization_barrier(jnp.sum(moved, axis=0))
    gram = jnp.dot(c_mat, b_mat.T, preferred_element_type=jnp.float32)
    decay = pair_decay(cumul)
    full_w = gram[None] * decay * step_size.T[:, None, :]
    weights_mat = full_w.astype(jnp.bfloat16)
    d_heads_b = d_heads.astype(jnp.bfloat16)
    d_x = d_x + mixing('hts,thp->shp', weights_mat, d_heads_b)
    d_weights = mixing('thp,shp->hts', d_heads_b, xheads_b)
    product = d_weights * full_w
    d_cumul = d_cumul + lax.optimization_barrier(jnp.sum(product, axis=2)).T - lax.optimization_barrier(jnp.sum(product, axis=1)).T
    d_step = d_step + lax.optimization_barrier(jnp.sum(d_weights * gram[None] * decay, axis=1)).T
    d_gram = lax.optimization_barrier(jnp.sum(d_weights * decay * step_size.T[:, None, :], axis=0)).astype(jnp.bfloat16)
    d_cmat = d_cmat + jnp.dot(d_gram, b_mat, preferred_element_type=jnp.float32)
    d_bmat = d_bmat + jnp.dot(d_gram.T, c_mat, preferred_element_type=jnp.float32)
    d_cumul = d_cumul.at[length - 1].add(d_last)
    d_rate_term = jnp.flip(jnp.cumsum(jnp.flip(d_cumul, 0), axis=0), 0)
    rate = -jnp.exp(log_rate)
    d_step = d_step + d_rate_term * rate
    d_log_rate = lax.optimization_barrier(jnp.sum(d_rate_term * step_size, axis=0)) * rate
    d_raw = d_step * jax.nn.sigmoid(step_raw + step_bias)
    d_bias = lax.optimization_barrier(jnp.sum(d_raw, axis=0))
    d_full_bc = jnp.concatenate([d_bmat, d_cmat], axis=1)
    return (d_x.reshape(length, -1), d_full_bc, d_raw, d_log_rate, d_bias)

def conv_inputs(d_zpart, dpad_x, dpad_bc, after, inner_local, kernel):
    rows = dpad_x.shape[-2] - kernel + 1
    front_x = jnp.zeros_like(dpad_x[..., :rows - kernel + 1, :])
    front_bc = jnp.zeros_like(dpad_bc[..., :rows - kernel + 1, :])
    d_pre_x = dpad_x[..., kernel - 1:, :] + jnp.concatenate([front_x, after[..., :inner_local]], axis=-2)
    d_pre_bc = dpad_bc[..., kernel - 1:, :] + jnp.concatenate([front_bc, after[..., inner_local:]], axis=-2)
    d_zx = jnp.concatenate([d_zpart, d_pre_x], axis=-1).astype(jnp.bfloat16)
    return (d_zx, d_pre_bc.astype(jnp.bfloat16))

def group_forward(stream, before, state, current):
    gain, weight_zx, weight_bc, weight_step, step_bias, log_rate, skip_gain, taps_x, offset_x, taps_bc, offset_bc, gate_gain, weight_out = current
    inner = weight_zx.shape[-1]
    kernel = taps_x.shape[0]
    length = stream.shape[0]
    normed, inv_rms = norm_forward(stream, gain)
    proj_zx, pre_bc, step_raw = project_in(normed, weight_zx, weight_bc, weight_step)
    pad_x = jnp.concatenate([before[:, :inner], proj_zx[:, inner:]], axis=0)
    pad_bc = jnp.concatenate([before[:, inner:], pre_bc], axis=0)
    conv_xv = silu_of(conv_forward(pad_x, taps_x, offset_x)).astype(jnp.bfloat16)
    full_bc = silu_of(conv_forward(pad_bc, taps_bc, offset_bc)).astype(jnp.bfloat16)
    step_size, cumul = decay_parts(step_raw, step_bias, log_rate)
    intra, end_state = ssd_group(conv_xv, full_bc, step_size, cumul)
    mixed, carried = ssd_output(intra, state, conv_xv, full_bc, cumul, skip_gain)
    gated, squares = gate_local(mixed, proj_zx)
    gate_o, inv_gate = gate_apply(gated, squares, gate_gain, inner)
    new_stream = stream + jnp.dot(gate_o, weight_out, preferred_element_type=jnp.float32)
    next_before = jnp.concatenate([proj_zx[length - kernel + 1:, inner:], pre_bc[length - kernel + 1:]], axis=1)
    next_state = jnp.exp(cumul[-1])[:, None, None] * state + end_state
    saved = (stream, normed, inv_rms, proj_zx, pad_x, pad_bc, conv_xv, full_bc, step_raw, step_size, cumul, state, carried, mixed, gated, inv_gate, gate_o)
    return (new_stream, next_before, next_state, saved)

def group_backward(grad, after, later_grad, saved, current):
    gain, weight_zx, weight_bc, weight_step, step_bias, log_rate, skip_gain, taps_x, offset_x, taps_bc, offset_bc, gate_gain, weight_out = current
    stream, normed, inv_rms, proj_zx, pad_x, pad_bc, conv_xv, full_bc, step_raw, step_size, cumul, state_in, carried, mixed, gated, inv_gate, gate_o = saved
    inner = weight_zx.shape[-1]
    width = weight_zx.shape[0]
    kernel = taps_x.shape[0]
    grad_b = grad.astype(jnp.bfloat16)
    d_wout = jnp.dot(gate_o.T, grad_b, preferred_element_type=jnp.float32)
    d_gate_o = jnp.dot(grad_b, weight_out.T, preferred_element_type=jnp.float32)
    scaled = d_gate_o * gate_gain
    d_gain_gate = lax.optimization_barrier(jnp.sum(d_gate_o * gated * inv_gate, axis=0))
    dots = lax.optimization_barrier(jnp.sum(scaled * gated, axis=-1))
    d_gated = gate_back(scaled, gated, inv_gate, dots, inner)
    d_mixed, d_zpart = gate_inputs(d_gated, mixed, proj_zx)
    d_x, d_cumul, d_cmat, d_state, d_skip = ssd_back_carried(d_mixed, conv_xv, full_bc, cumul, carried, state_in, skip_gain)
    d_x, d_full_bc, d_raw, d_rate, d_bias = ssd_back_rest(d_mixed, d_x, d_cumul, d_cmat, later_grad, state_in, conv_xv, full_bc, step_raw, step_size, cumul, step_bias, log_rate)
    dpad_x, d_taps_x, d_offset_x = conv_backward(d_x, pad_x, taps_x, offset_x)
    dpad_bc, d_taps_bc, d_offset_bc = conv_backward(d_full_bc, pad_bc, taps_bc, offset_bc)
    edges = jnp.concatenate([dpad_x[:kernel - 1], dpad_bc[:kernel - 1]], axis=1)
    d_zx, d_pre_bc = conv_inputs(d_zpart, dpad_x, dpad_bc, after, inner, kernel)
    d_raw_b = d_raw.astype(jnp.bfloat16)
    d_normed = jnp.dot(d_zx, weight_zx.reshape(width, -1).T, preferred_element_type=jnp.float32)
    d_normed = d_normed + jnp.dot(d_pre_bc, weight_bc.T, preferred_element_type=jnp.float32)
    d_normed = d_normed + jnp.dot(d_raw_b, weight_step.T, preferred_element_type=jnp.float32)
    d_wzx = jnp.dot(normed.T, d_zx, preferred_element_type=jnp.float32).reshape(width, 2, inner)
    d_wbc = jnp.dot(normed.T, d_pre_bc, preferred_element_type=jnp.float32)
    d_wstep = jnp.dot(normed.T, d_raw_b, preferred_element_type=jnp.float32)
    grad_in, d_gain_norm = norm_back(grad, d_normed, stream, inv_rms, gain)
    new_later = d_state + jnp.exp(cumul[-1])[:, None, None] * later_grad
    parts = (d_gain_norm, d_wzx, d_wbc, d_wstep, d_bias, d_rate, d_skip, d_taps_x, d_offset_x, d_taps_bc, d_offset_bc, d_gain_gate, d_wout)
    return (grad_in, edges, new_later, parts)

def reference(tokens, cotangent, norm_gain, weight_zx, weight_bc, weight_step, step_bias, log_rate, skip_gain, taps_x, offset_x, taps_bc, offset_bc, gate_gain, weight_out):
    weights = (norm_gain, weight_zx, weight_bc, weight_step, step_bias, log_rate, skip_gain, taps_x, offset_x, taps_bc, offset_bc, gate_gain, weight_out)
    kernel = taps_x.shape[1]
    edge_width = INNER + 2 * STATE
    groups = LEN // GROUP

    def one_sequence(totals, pair):
        sequence, grad_seq = pair
        stream = sequence.reshape(groups, GROUP, D)
        saves = []
        for layer in range(LAYERS):
            current = tuple((member[layer] for member in weights))

            def forward_step(carry, block):
                before, state = carry
                new_block, next_before, next_state, saved = group_forward(block, before, state, current)
                return ((next_before, next_state), (new_block, saved))
            start = (jnp.zeros((kernel - 1, edge_width), jnp.bfloat16), jnp.zeros((HEADS, HEADDIM, STATE), jnp.float32))
            ignored, (stream, saved) = lax.scan(forward_step, start, stream)
            saves.append(saved)
        grad = grad_seq.reshape(groups, GROUP, D)
        new_totals = list(totals)
        for layer in reversed(range(LAYERS)):
            current = tuple((member[layer] for member in weights))

            def backward_step(carry, inputs):
                after, later_grad = carry
                block_grad, saved = inputs
                grad_in, edges, new_later, parts = group_backward(block_grad, after, later_grad, saved, current)
                return ((edges, new_later), (grad_in, parts))
            start = (jnp.zeros((kernel - 1, edge_width), jnp.float32), jnp.zeros((HEADS, HEADDIM, STATE), jnp.float32))
            ignored, (grad, parts) = lax.scan(backward_step, start, (grad, saves[layer]), reverse=True)
            new_totals = [total.at[layer].add(lax.optimization_barrier(jnp.sum(part, axis=0))) for total, part in zip(new_totals, parts)]
        return (tuple(new_totals), (stream.reshape(LEN, D), grad.reshape(LEN, D)))
    start = tuple((jnp.zeros(member.shape, jnp.float32) for member in weights))
    totals, (output, grad_tokens) = lax.scan(one_sequence, start, (tokens, cotangent))
    return (output, grad_tokens, totals[0], totals[1], totals[2], totals[3], totals[4], totals[5], totals[6], totals[7], totals[8], totals[9], totals[10], totals[11], totals[12])
```

```python
import jax
import jax.numpy as jnp
from jax import lax
from jax.experimental import pallas as pl
from jax.experimental.pallas import tpu as pltpu
from jax.sharding import PartitionSpec as P

INTERPRET = False

F32 = jnp.float32
BF16 = jnp.bfloat16
EPS = 1e-05
HALO = 8
MASKED = -1e30


def nn(a, b):
    return lax.dot_general(a, b, (((1,), (0,)), ((), ())), preferred_element_type=F32)


def nt(a, b):
    return lax.dot_general(a, b, (((1,), (1,)), ((), ())), preferred_element_type=F32)


def tn(a, b):
    return lax.dot_general(a, b, (((0,), (0,)), ((), ())), preferred_element_type=F32)


def parts_of(value, count):
    pieces = []
    for _ in range(count):
        piece = value.astype(BF16)
        pieces.append(piece)
        value = value - piece.astype(F32)
    return pieces


def split_dot(dot, left, right, count, on_left=True):
    total = None
    for piece in parts_of(left if on_left else right, count):
        term = dot(piece, right) if on_left else dot(left, piece)
        total = term if total is None else total + term
    return total


def head_map(heads, channels):
    size = channels // heads
    rows = lax.broadcasted_iota(jnp.int32, (heads, channels), 0)
    cols = lax.broadcasted_iota(jnp.int32, (heads, channels), 1)
    inside = (cols >= rows * size) & (cols < (rows + 1) * size)
    return jnp.where(inside, 1.0, 0.0).astype(BF16)


def expand(value, spread):
    return split_dot(nn, value, spread, 2)


def head_sum(value, spread):
    return split_dot(nt, value, spread, 2)


def eye(size):
    rows = lax.broadcasted_iota(jnp.int32, (size, size), 0)
    cols = lax.broadcasted_iota(jnp.int32, (size, size), 1)
    return jnp.where(rows == cols, 1.0, 0.0).astype(BF16)


def triangle(size, upper):
    rows = lax.broadcasted_iota(jnp.int32, (size, size), 0)
    cols = lax.broadcasted_iota(jnp.int32, (size, size), 1)
    keep = cols >= rows if upper else rows >= cols
    return jnp.where(keep, 1.0, 0.0).astype(BF16)


def turned(value):
    return split_dot(nt, eye(value.shape[1]), value, 3, on_left=False)


def turned_back(value):
    return split_dot(nt, eye(value.shape[1]), value, 3, on_left=False)


def sigmoid(value):
    return jax.nn.sigmoid(value)


def softplus(value):
    return jnp.maximum(value, 0.0) + jnp.log1p(jnp.exp(-jnp.abs(value)))


def conv_sum(scratch, taps, offset, length):
    kernel = taps.shape[0]
    first = HALO - kernel + 1
    total = offset + taps[0:1] * scratch[first : first + length]
    for k in range(1, kernel):
        total = total + taps[k : k + 1] * scratch[first + k : first + k + length]
    return total


def square_column(own_rows, other_rows):
    size = own_rows.shape[1]
    own = nt(eye(size), own_rows)
    other = nt(eye(size), other_rows)
    return (own[:, 0:1] + own[:, 1:2]) + (other[:, 0:1] + other[:, 1:2])


def inv_gate_of(own_rows, other_rows, inner):
    return lax.rsqrt(square_column(own_rows, other_rows) / inner + EPS)


def call(body, out_shape, operands, specs=None, scratch=(), name=None):
    full = pl.BlockSpec(memory_space=pltpu.VMEM)
    in_specs = [full] * len(operands) if specs is None else specs
    return pl.pallas_call(
        body,
        out_shape=out_shape,
        grid=(1,),
        in_specs=in_specs,
        out_specs=jax.tree.map(lambda _: full, out_shape),
        scratch_shapes=list(scratch),
        interpret=INTERPRET,
        name=name,
    )(*operands)


VM = pl.BlockSpec(memory_space=pltpu.VMEM)
SM = pl.BlockSpec(memory_space=pltpu.SMEM)


def layer_block(array, layer):
    rest = array.shape[1:]
    return pl.BlockSpec((None,) + rest, lambda *_: (layer,) + (0,) * len(rest))


def shape_of(shape, dtype):
    return jax.ShapeDtypeStruct(shape, dtype)


def enter_body(layer, first, inner, refs):
    if first:
        (head_ref, tokens_ref, halo_ref), refs = (refs[:3], refs[3:])
    else:
        (head_ref, tokens_ref, halo_ref, own_ref, other_ref, same_ref, cross_ref), refs = (
            refs[:7],
            refs[7:],
        )
    (gain_ref, wzx_ref, wown_ref, wpart_ref, wstep_ref, bias_ref, rate_ref), refs = (refs[:7], refs[7:])
    (taps_x_ref, off_x_ref, taps_own_ref, off_own_ref, bc_part_ref), refs = (refs[:5], refs[5:])
    outs, refs = refs[: 11 if first else 12], refs[11 if first else 12 :]
    xs_ref, bs_ref = refs
    length = outs[1].shape[0]
    state = wown_ref.shape[1]
    if first:
        own = tokens_ref[...]
        halo = halo_ref[...]
        (normed_ref, z_ref, x_ref, bc_ref, conv_ref, full_ref, step_ref, cumul_ref, raw_ref, st_ref, decay_ref) = outs
    else:
        (normed_ref, z_ref, x_ref, bc_ref, conv_ref, full_ref, step_ref, cumul_ref, raw_ref, st_ref, decay_ref, stream_ref) = outs
        pay_a, pay_b = own_ref[...].astype(F32), other_ref[...].astype(F32)
        inv = inv_gate_of(
            pay_a[length:, :length].astype(BF16), pay_b[length:, :length].astype(BF16), inner
        )
        own = tokens_ref[0:length] + inv * (pay_a[:length] + pay_b[:length])
        near_a, near_b = same_ref[...].astype(F32), cross_ref[...].astype(F32)
        inv = inv_gate_of(
            near_a[HALO:, :length].astype(BF16), near_b[HALO:, :length].astype(BF16), inner
        )[length - HALO :]
        halo = halo_ref[...] + inv * (near_a[:HALO] + near_b[:HALO])
        stream_ref[0:length] = own
        stream_ref[length:] = halo
    ext = jnp.concatenate([own, halo], axis=0)
    inv_rms = lax.rsqrt(jnp.mean(ext * ext, axis=1, keepdims=True) + EPS)
    normed = (ext * inv_rms * gain_ref[layer : layer + 1]).astype(BF16)
    normed_ref[...] = normed
    z_ref[...] = nn(normed[:length], wzx_ref[0]).astype(BF16)
    x_ext = nn(normed, wzx_ref[1]).astype(BF16)
    x_ref[...] = x_ext
    xs_ref[0:HALO] = x_ext[length:].astype(F32)
    xs_ref[HALO:] = x_ext[:length].astype(F32)
    before = conv_sum(xs_ref, taps_x_ref[...], off_x_ref[layer : layer + 1], length)
    conv_x = (before * sigmoid(before)).astype(BF16)
    conv_ref[...] = conv_x
    bc_own = nn(normed, wown_ref[...]).astype(BF16)
    bc_part = nn(normed, wpart_ref[...]).astype(BF16)
    bc_ref[:, 0:state] = bc_own
    bc_ref[:, state:] = bc_part
    bs_ref[0:HALO, 0:state] = bc_own[length:].astype(F32)
    bs_ref[0:HALO, state:] = bc_part[length:].astype(F32)
    bs_ref[HALO:, 0:state] = bc_own[:length].astype(F32)
    bs_ref[HALO:, state:] = bc_part[:length].astype(F32)
    kernel = taps_own_ref.shape[0]
    taps_bc = jnp.concatenate([taps_own_ref[...], bc_part_ref[0:kernel]], axis=1)
    off_bc = jnp.concatenate([off_own_ref[layer : layer + 1], bc_part_ref[kernel : kernel + 1]], axis=1)
    before = conv_sum(bs_ref, taps_bc, off_bc, length)
    conv_bc = before * sigmoid(before)
    is_first = head_ref[0] == 0
    b_mat = jnp.where(is_first, conv_bc[:, 0:state], conv_bc[:, state:]).astype(BF16)
    c_mat = jnp.where(is_first, conv_bc[:, state:], conv_bc[:, 0:state]).astype(BF16)
    full_ref[:, 0:state] = b_mat
    full_ref[:, state:] = c_mat
    raw = nt(normed[:length], wstep_ref[...]) + bias_ref[layer : layer + 1]
    raw_ref[...] = raw
    step = softplus(raw)
    scaled = step * -jnp.exp(rate_ref[layer : layer + 1])
    cumul = split_dot(nn, triangle(length, False), scaled, 3, on_left=False)
    step_ref[...] = step
    cumul_ref[...] = cumul
    last = cumul[length - 1 :]
    spread = head_map(step.shape[1], conv_x.shape[1])
    factor = expand(step * jnp.exp(last - cumul), spread)
    scaled_x = (conv_x.astype(F32) * factor).astype(BF16)
    st_ref[...] = tn(b_mat, scaled_x).astype(BF16)
    decay_ref[...] = expand(jnp.broadcast_to(jnp.exp(last), (HALO, last.shape[1])), spread)


def pair_of(value, index, width):
    return value[:, index * width : (index + 1) * width]


def stacked_pair(pair, size):
    lanes = lax.broadcasted_iota(jnp.int32, pair.shape, 1)
    zero = jnp.zeros_like(pair)
    per = pair.shape[1] // size
    return [jnp.where((lanes >= i * size) & (lanes < (i + 1) * size), pair, zero) for i in range(per)]


def intra_body(refs):
    conv_ref, full_ref, step_ref, cumul_ref, intra_ref = refs
    length, heads = step_ref.shape
    channels = conv_ref.shape[1]
    size = channels // heads
    state = full_ref.shape[1] // 2
    per = max(1, 128 // size)
    b_mat, c_mat = full_ref[:, 0:state], full_ref[:, state:]
    gram = nt(c_mat, b_mat)
    cumul = cumul_ref[...]
    step_rows = turned(step_ref[...])
    cumul_rows = turned(cumul)
    rows = lax.broadcasted_iota(jnp.int32, (length, length), 0)
    cols = lax.broadcasted_iota(jnp.int32, (length, length), 1)
    lower = rows >= cols
    for j in range(heads // per):
        weights = []
        for h in range(j * per, (j + 1) * per):
            gap = cumul[:, h : h + 1] - cumul_rows[h : h + 1]
            decay = jnp.exp(jnp.where(lower, gap, MASKED))
            weights.append((gram * decay * step_rows[h : h + 1]).astype(BF16))
        blocks = stacked_pair(conv_ref[:, j * per * size : (j + 1) * per * size], size)
        intra_ref[:, j * per * size : (j + 1) * per * size] = nn(
            jnp.concatenate(weights, axis=1), jnp.concatenate(blocks, axis=0)
        )


def leave_body(layer, refs):
    (st_ref, intra_ref, conv_ref, full_ref, cumul_ref, z_ref, skip_ref, gain_ref, wout_ref) = refs[:9]
    mixed_ref, pay_ref, near_ref = refs[9:]
    length, channels = conv_ref.shape
    heads = cumul_ref.shape[1]
    state = full_ref.shape[1] // 2
    spread = head_map(heads, channels)
    carried = nn(full_ref[:, state:], st_ref[...])
    grow = expand(jnp.exp(cumul_ref[...]), spread)
    skip = expand(jnp.broadcast_to(skip_ref[layer : layer + 1], (HALO, heads)), spread)[0:1]
    mixed = intra_ref[...] + grow * carried + skip * conv_ref[...].astype(F32)
    mixed_ref[...] = mixed
    z = z_ref[...].astype(F32)
    gated = mixed * (z * sigmoid(z))
    part = nn((gated * gain_ref[layer : layer + 1]).astype(BF16), wout_ref[...]).astype(BF16)
    squares = split_dot(nt, jnp.ones((HALO, channels), BF16), gated * gated, 3, on_left=False)
    high = squares.astype(BF16).astype(F32)
    row = lax.broadcasted_iota(jnp.int32, squares.shape, 0)
    lines = jnp.where(row == 0, high, jnp.where(row == 1, squares - high, 0.0))
    width = part.shape[1]
    if width > length:
        lines = jnp.concatenate([lines, jnp.zeros((HALO, width - length), F32)], axis=1)
    lines = lines.astype(BF16)
    pay_ref[0:length] = part
    pay_ref[length:] = lines
    near_ref[...] = jnp.concatenate([part[length - HALO :].astype(F32), lines.astype(F32)], axis=0).astype(BF16)


def merged_grad(grad, own, other, same, cross, ext, gain):
    length = grad.shape[0]
    d_normed = own.astype(F32) + other.astype(F32)
    tail = d_normed[length - HALO :] + (same.astype(F32) + cross.astype(F32))
    d_normed = jnp.concatenate([d_normed[: length - HALO], tail], axis=0)
    inv_rms = lax.rsqrt(jnp.mean(ext * ext, axis=1, keepdims=True) + EPS)
    scaled = d_normed * gain
    pull = jnp.mean(scaled * ext, axis=1, keepdims=True)
    return grad + inv_rms * scaled - ext * (inv_rms * inv_rms * inv_rms) * pull


def gate_body(layer, last, inner, refs):
    if last:
        (cot_ref, stream_ref), refs = refs[:2], refs[2:]
    else:
        (cot_ref, down_ref, up_ref, same_ref, cross_ref, later_ref, norm_ref), refs = refs[:7], refs[7:]
    (own_ref, other_ref, z_ref, mixed_ref, full_ref, cumul_ref, conv_ref, gain_ref, wout_ref), refs = refs[:9], refs[9:]
    out_ref, state_ref, dmixed_ref, dz_ref, gate_ref, gradb_ref, sums_ref, dskip_ref = refs
    length, channels = mixed_ref.shape
    state = full_ref.shape[1] // 2
    pay_a, pay_b = own_ref[...].astype(F32), other_ref[...].astype(F32)
    inv = inv_gate_of(pay_a[length:, :length].astype(BF16), pay_b[length:, :length].astype(BF16), inner)
    whole = pay_a[:length] + pay_b[:length]
    if last:
        grad = cot_ref[...]
        out_ref[...] = stream_ref[0:length] + inv * whole
    else:
        grad = merged_grad(
            cot_ref[...], down_ref[...], up_ref[...], same_ref[...], cross_ref[...],
            later_ref[0:length], norm_ref[layer + 1 : layer + 2],
        )
        out_ref[...] = grad
    grad_b = grad.astype(BF16)
    gradb_ref[...] = grad_b
    gain = gain_ref[layer : layer + 1]
    d_gate = nt(grad_b, wout_ref[...])
    z = z_ref[...].astype(F32)
    sigma = sigmoid(z)
    silu = z * sigma
    mixed = mixed_ref[...]
    gated = mixed * silu
    unit = gated * inv
    gate_ref[...] = (unit * gain).astype(BF16)
    sums_ref[...] = jnp.broadcast_to(jnp.sum(d_gate * unit, axis=0, keepdims=True), sums_ref.shape)
    dots = jnp.sum(grad_b.astype(F32) * whole, axis=1, keepdims=True)
    d_gated = inv * (d_gate * gain) - gated * (inv * inv * inv) * (dots / inner)
    d_mixed = d_gated * silu
    dmixed_ref[...] = d_mixed
    dz_ref[...] = (d_gated * mixed * sigma * (1.0 + z * (1.0 - sigma))).astype(BF16)
    spread = head_map(cumul_ref.shape[1], channels)
    grow = expand(jnp.exp(cumul_ref[...]), spread)
    state_ref[...] = tn(full_ref[:, state:], (d_mixed * grow).astype(BF16)).astype(BF16)
    d_skip = jnp.sum(d_mixed * conv_ref[...].astype(F32), axis=0, keepdims=True)
    dskip_ref[...] = head_sum(jnp.broadcast_to(d_skip, (HALO, channels)), spread)


def pairs_body(layer, refs):
    (dmixed_ref, conv_ref, full_ref, step_ref, cumul_ref, st_ref, skip_ref) = refs[:7]
    dx_ref, dbc_ref, dstep_ref, dcumul_ref, lines_ref = refs[7:]
    length, heads = step_ref.shape
    channels = conv_ref.shape[1]
    size = channels // heads
    state = full_ref.shape[1] // 2
    per = max(1, 128 // size)
    spread = head_map(heads, channels)
    b_mat, c_mat = full_ref[:, 0:state], full_ref[:, state:]
    d_mixed = dmixed_ref[...]
    cumul = cumul_ref[...]
    step = step_ref[...]
    grow = expand(jnp.exp(cumul), spread)
    moved = d_mixed * grow
    st = st_ref[...]
    d_c = nt(moved.astype(BF16), st)
    d_cumul = head_sum(moved * nn(c_mat, st), spread)
    skip = expand(jnp.broadcast_to(skip_ref[layer : layer + 1], (HALO, heads)), spread)[0:1]
    gram = nt(b_mat, c_mat)
    cumul_rows = turned(cumul)
    rows = lax.broadcasted_iota(jnp.int32, (length, length), 0)
    cols = lax.broadcasted_iota(jnp.int32, (length, length), 1)
    upper = cols >= rows
    lane = lax.broadcasted_iota(jnp.int32, (length, heads), 1)
    d_gram = jnp.zeros((length, length), F32)
    d_step = jnp.zeros((length, heads), F32)
    lines_ref[...] = jnp.zeros(lines_ref.shape, F32)
    for j in range(heads // per):
        here = slice(j * per * size, (j + 1) * per * size)
        d_pair = d_mixed[:, here]
        d_pair_b = d_pair.astype(BF16)
        d_blocks = stacked_pair(d_pair_b, size)
        x_blocks = stacked_pair(conv_ref[:, here], size)
        weights = []
        for i in range(per):
            h = j * per + i
            gap = cumul_rows[h : h + 1] - cumul[:, h : h + 1]
            decay = jnp.exp(jnp.where(upper, gap, MASKED))
            step_col = step[:, h : h + 1]
            shaded = decay * step_col
            weights.append((gram * shaded).astype(BF16))
            d_weights = nt(x_blocks[i], d_pair_b)
            d_gram = d_gram + d_weights * shaded
            slope = d_weights * (decay * gram)
            d_step = jnp.where(lane == h, jnp.sum(slope, axis=1, keepdims=True), d_step)
            lines_ref[h : h + 1] = jnp.sum(slope * step_col, axis=0, keepdims=True)
        dx_ref[:, here] = skip[:, here] * d_pair + nn(
            jnp.concatenate(weights, axis=1), jnp.concatenate(d_blocks, axis=0)
        )
    d_gram_b = d_gram.astype(BF16)
    dbc_ref[:, 0:state] = nn(d_gram_b, c_mat)
    dbc_ref[:, state:] = d_c + tn(d_gram_b, b_mat)
    dstep_ref[...] = d_step
    dcumul_ref[...] = d_cumul - step * d_step + turned_back(lines_ref[...])[:, :heads]


def pad_rows(scratch, value):
    length = value.shape[0]
    zero = jnp.zeros((HALO, value.shape[1]), F32)
    scratch[0:HALO] = zero
    scratch[HALO : HALO + length] = value
    scratch[HALO + length :] = zero


def conv_back(values, before, d_out, taps, padded, length):
    kernel = taps.shape[0]
    first = HALO - kernel + 1
    sigma = sigmoid(before)
    d_pre = d_out * sigma * (1.0 + before * (1.0 - sigma))
    d_taps = [
        jnp.sum(d_pre * values[first + k : first + k + length], axis=0, keepdims=True)
        for k in range(kernel)
    ]
    d_off = jnp.sum(d_pre, axis=0, keepdims=True)
    pad_rows(padded, d_pre)
    rows = length + HALO
    total = taps[0:1] * padded[kernel - 1 : kernel - 1 + rows]
    for k in range(1, kernel):
        total = total + taps[k : k + 1] * padded[kernel - 1 - k : kernel - 1 - k + rows]
    return jnp.concatenate([total[HALO:], total[:HALO]], axis=0), d_taps, d_off


def back_body(layer, refs):
    (head_ref, later_ref, st_ref, full_ref, conv_ref, step_ref, cumul_ref, raw_ref), refs = refs[:8], refs[8:]
    (rate_ref, dx_ref, dbc_ref, dstep_ref, dcumul_ref, dz_ref, x_ref, bc_ref, stream_ref), refs = refs[:9], refs[9:]
    (taps_x_ref, off_x_ref, taps_own_ref, off_own_ref, bc_part_ref), refs = refs[:5], refs[5:]
    (wzx_ref, wown_ref, wpart_ref, wstep_ref, sums_ref, dskip_ref), refs = refs[:6], refs[6:]
    (down_ref, near_ref, dxin_ref, dbcin_ref, dpart_ref, draw_ref, share_ref, small_ref), refs = refs[:8], refs[8:]
    xs_ref, bs_ref, xp_ref, bp_ref = refs
    length, heads = step_ref.shape
    channels = conv_ref.shape[1]
    state = full_ref.shape[1] // 2
    spread = head_map(heads, channels)
    later = later_ref[...]
    b_mat = full_ref[:, 0:state]
    cumul = cumul_ref[...]
    step = step_ref[...]
    last = cumul[length - 1 :]
    tail = jnp.exp(last - cumul)
    factor = step * tail
    wide = expand(factor, spread)
    conv_x = conv_ref[...].astype(F32)
    d_scaled = nn(b_mat, later)
    d_b = dbc_ref[:, 0:state] + nt((conv_x * wide).astype(BF16), later)
    d_c = dbc_ref[:, state:]
    d_x = dx_ref[...] + d_scaled * wide
    d_factor = head_sum(d_scaled * conv_x, spread)
    moved = d_factor * factor
    both = jnp.sum(later.astype(F32) * st_ref[...].astype(F32), axis=0, keepdims=True)
    d_last = jnp.exp(last) * head_sum(jnp.broadcast_to(both, (HALO, channels)), spread)[0:1]
    d_last = d_last + jnp.sum(moved, axis=0, keepdims=True)
    at_last = lax.broadcasted_iota(jnp.int32, (length, heads), 0) == length - 1
    d_cumul = dcumul_ref[...] - moved + jnp.where(at_last, d_last, 0.0)
    d_term = split_dot(nn, triangle(length, True), d_cumul, 3, on_left=False)
    rate = -jnp.exp(rate_ref[layer : layer + 1])
    d_step = dstep_ref[...] + d_factor * tail + d_term * rate
    d_rate = jnp.sum(d_term * step, axis=0, keepdims=True) * rate
    d_raw = d_step * sigmoid(raw_ref[...])
    d_bias = jnp.sum(d_raw, axis=0, keepdims=True)
    d_raw_b = d_raw.astype(BF16)
    draw_ref[...] = d_raw_b
    kernel = taps_x_ref.shape[0]
    xs_ref[0:HALO] = x_ref[length:].astype(F32)
    xs_ref[HALO:] = x_ref[:length].astype(F32)
    taps_x = taps_x_ref[...]
    before = conv_sum(xs_ref, taps_x, off_x_ref[layer : layer + 1], length)
    d_in, d_taps_x, d_off_x = conv_back(xs_ref, before, d_x, taps_x, xp_ref, length)
    d_in = d_in.astype(BF16)
    dxin_ref[...] = d_in
    is_first = head_ref[0] == 0
    d_conv = jnp.concatenate([jnp.where(is_first, d_b, d_c), jnp.where(is_first, d_c, d_b)], axis=1)
    bs_ref[0:HALO] = bc_ref[length:].astype(F32)
    bs_ref[HALO:] = bc_ref[:length].astype(F32)
    taps_bc = jnp.concatenate([taps_own_ref[...], bc_part_ref[0:kernel]], axis=1)
    off_bc = jnp.concatenate([off_own_ref[layer : layer + 1], bc_part_ref[kernel : kernel + 1]], axis=1)
    before = conv_sum(bs_ref, taps_bc, off_bc, length)
    d_bcin, d_taps_bc, d_off_bc = conv_back(bs_ref, before, d_conv, taps_bc, bp_ref, length)
    d_bcin = d_bcin.astype(BF16)
    dbcin_ref[...] = d_bcin[:, 0:state]
    dpart_ref[...] = d_bcin[:, state:]
    d_normed = (
        nt(d_in, wzx_ref[1]) + nt(d_bcin[:, 0:state], wown_ref[...]) + nt(d_bcin[:, state:], wpart_ref[...])
    )
    mine = d_normed[:length] + nt(dz_ref[...], wzx_ref[0]) + nn(d_raw_b, wstep_ref[...])
    near = d_normed[length:]
    down_ref[...] = mine.astype(BF16)
    near_ref[...] = near
    ext = stream_ref[...]
    inv_rms = lax.rsqrt(jnp.mean(ext * ext, axis=1, keepdims=True) + EPS)
    unit = ext * inv_rms
    d_gain = jnp.sum(mine * unit[:length], axis=0, keepdims=True)
    d_gain = d_gain + jnp.sum(near * unit[length:], axis=0, keepdims=True)
    share_ref[...] = jnp.zeros(share_ref.shape, F32)
    share_ref[0:1] = d_gain
    for k in range(kernel):
        share_ref[1 + k : 2 + k, 0 : 2 * state] = d_taps_bc[k]
    share_ref[1 + kernel : 2 + kernel, 0 : 2 * state] = d_off_bc
    small_ref[...] = jnp.zeros(small_ref.shape, F32)
    small_ref[0:1] = sums_ref[0:1]
    for k in range(kernel):
        small_ref[1 + k : 2 + k] = d_taps_x[k]
    small_ref[1 + kernel : 2 + kernel] = d_off_x
    small_ref[2 + kernel : 3 + kernel, 0:heads] = d_bias
    small_ref[2 + kernel : 3 + kernel, 128 : 128 + heads] = d_rate
    small_ref[2 + kernel : 3 + kernel, 256 : 256 + heads] = dskip_ref[0:1]


def early_body(refs):
    normed_ref, dz_ref, gradb_ref, gate_ref, out_ref = refs
    length, width = gradb_ref.shape
    channels = dz_ref.shape[1]
    out_ref[:, 0:channels] = tn(normed_ref[0:length], dz_ref[...]).astype(BF16)
    out_ref[:, channels:] = tn(gradb_ref[...], gate_ref[...]).astype(BF16)


def late_body(refs):
    normed_ref, dxin_ref, draw_ref, out_ref = refs
    length, heads = draw_ref.shape
    channels = dxin_ref.shape[1]
    normed = normed_ref[...]
    out_ref[:, 0:channels] = tn(normed, dxin_ref[...]).astype(BF16)
    out_ref[:, channels:] = jnp.zeros((out_ref.shape[0], 128), BF16)
    out_ref[:, channels : channels + heads] = tn(normed[:length], draw_ref[...]).astype(BF16)


def bc_body(refs):
    normed_ref, own_ref, other_ref, out_ref = refs
    total = (own_ref[...].astype(F32) + other_ref[...].astype(F32)).astype(BF16)
    out_ref[...] = tn(normed_ref[...], total).astype(BF16)


def final_body(layer, refs):
    cot_ref, down_ref, up_ref, same_ref, cross_ref, stream_ref, norm_ref, out_ref = refs
    length = cot_ref.shape[0]
    out_ref[...] = merged_grad(
        cot_ref[...], down_ref[...], up_ref[...], same_ref[...], cross_ref[...],
        stream_ref[0:length], norm_ref[layer : layer + 1],
    )


def starred(body, *fixed):
    return lambda *refs: body(*fixed, refs)


def flip(value, axis, bit):
    count = lax.axis_size(axis)
    return lax.ppermute(value, axis, [(i, i ^ bit) for i in range(count)])


def to_next(value, distance, cross):
    seqs, heads = lax.axis_size("seq"), lax.axis_size("head")
    route = []
    for s in range(seqs):
        for h in range(heads):
            if 0 <= s + distance < seqs:
                to = heads - 1 - h if cross else h
                route.append((s * heads + h, (s + distance) * heads + to))
    return lax.ppermute(value, ("seq", "head"), route)


def bits_of(axis):
    return [1 << k for k in range(lax.axis_size(axis).bit_length() - 1)]


def summed(value):
    for axis in ("batch", "seq"):
        assert lax.axis_size(axis) & (lax.axis_size(axis) - 1) == 0
    stages = [("batch", 1)] + [("seq", b) for b in bits_of("seq")] + [("batch", b) for b in bits_of("batch")[1:]]
    for axis, bit in stages:
        value = value + flip(value, axis, bit)
    return value


def scattered(value):
    batches, seqs = lax.axis_size("batch"), lax.axis_size("seq")
    rows, width = value.shape
    block = rows // (batches * seqs)
    stages = [("batch", 1)] + [("seq", b) for b in bits_of("seq")] + [("batch", b) for b in bits_of("batch")[1:]]
    dims = [("batch", b) for b in reversed(bits_of("batch"))] + [("seq", b) for b in reversed(bits_of("seq"))]
    held = value.reshape((2,) * len(dims) + (block, width))
    for axis, bit in stages:
        place = dims.index((axis, bit))
        mine = (lax.axis_index(axis) // bit) % 2
        keep = lax.dynamic_index_in_dim(held, mine, place, keepdims=False)
        send = lax.dynamic_index_in_dim(held, 1 - mine, place, keepdims=False).astype(BF16)
        held = keep.astype(F32) + flip(send, axis, bit).astype(F32)
        dims.pop(place)
    return held


def entering(total_decay, state, reverse):
    count = lax.axis_size("seq")
    if count == 2:
        return lax.ppermute(state, "seq", [(1, 0)] if reverse else [(0, 1)])
    index = lax.axis_index("seq")
    states = lax.all_gather(state, "seq")
    decays = lax.all_gather(total_decay.astype(BF16), "seq").astype(F32)
    held = jnp.zeros(state.shape, F32)
    for k in range(count):
        at = count - 1 - k if reverse else k
        reached = at > index if reverse else at < index
        new = decays[at] * held + states[at].astype(F32)
        held = jnp.where(reached, new, held)
    return held.astype(BF16)


def body(
    tokens,
    cotangent,
    norm_gain,
    weight_zx,
    weight_bc,
    weight_step,
    step_bias,
    log_rate,
    skip_gain,
    taps_x,
    offset_x,
    taps_bc,
    offset_bc,
    gate_gain,
    weight_out,
):
    layers, width, _, channels = weight_zx.shape
    kernel = taps_x.shape[1]
    length = tokens.shape[1]
    heads = weight_step.shape[2]
    state = weight_bc.shape[2]
    assert lax.axis_size("head") == 2
    inner = float(channels * lax.axis_size("head"))
    head = lax.axis_index("head").astype(jnp.int32).reshape(1)
    tokens = tokens.reshape(length, width)
    grad = cotangent.reshape(length, width)

    halo = to_next(tokens[length - HALO :], 1, False)
    w_part = [flip(weight_bc[layer], "head", 1) for layer in range(layers)]
    bc_part = flip(jnp.concatenate([taps_bc, offset_bc[:, None]], axis=1), "head", 1)
    w_zx = [jnp.transpose(weight_zx[layer], (1, 0, 2)) for layer in range(layers)]
    w_step = jnp.transpose(weight_step, (0, 2, 1))

    rows = length + HALO
    saves = []
    stream = jnp.concatenate([tokens, halo], axis=0)
    arrival = None
    for layer in range(layers):
        outs = [
            shape_of((rows, width), BF16),
            shape_of((length, channels), BF16),
            shape_of((rows, channels), BF16),
            shape_of((rows, 2 * state), BF16),
            shape_of((length, channels), BF16),
            shape_of((length, 2 * state), BF16),
            shape_of((length, heads), F32),
            shape_of((length, heads), F32),
            shape_of((length, heads), F32),
            shape_of((state, channels), BF16),
            shape_of((HALO, channels), F32),
        ]
        operands = [head, tokens, halo]
        specs = [SM, VM, VM]
        if layer:
            operands = [head, stream, stream[length:]] + list(arrival)
            specs = [SM] + [VM] * (len(operands) - 1)
            outs.append(shape_of((rows, width), F32))
        operands += [norm_gain, w_zx[layer], weight_bc, w_part[layer], w_step, step_bias, log_rate]
        specs += [VM, VM, layer_block(weight_bc, layer), VM, layer_block(w_step, layer), VM, VM]
        operands += [taps_x, offset_x, taps_bc, offset_bc, bc_part]
        specs += [layer_block(taps_x, layer), VM, layer_block(taps_bc, layer), VM, layer_block(bc_part, layer)]
        got = call(
            starred(enter_body, layer, layer == 0, inner),
            tuple(outs),
            operands,
            specs,
            [pltpu.VMEM((rows, channels), F32), pltpu.VMEM((rows, 2 * state), F32)],
            name=f"enter{layer}",
        )
        if layer:
            stream = got[11]
        normed, z, x_ext, bc_ext, conv_x, full_bc, step, cumul, raw, end_state, decay = got[:11]
        state_in = entering(decay[0:1], end_state, False)
        intra = call(
            starred(intra_body),
            shape_of((length, channels), F32),
            [conv_x, full_bc, step, cumul],
            name=f"intra{layer}",
        )
        mixed, pay, near = call(
            starred(leave_body, layer),
            (shape_of((length, channels), F32), shape_of((rows, width), BF16), shape_of((2 * HALO, width), BF16)),
            [state_in, intra, conv_x, full_bc, cumul, z, skip_gain, gate_gain, weight_out],
            [VM] * 8 + [layer_block(weight_out, layer)],
            name=f"leave{layer}",
        )
        other = flip(pay, "head", 1)
        if layer + 1 < layers:
            arrival = (pay, other, to_next(near, 1, False), to_next(near, 1, True))
        saves.append((stream, normed, z, x_ext, bc_ext, conv_x, full_bc, step, cumul, raw, state_in, decay, mixed, pay, other))

    early, late, bc_grad, share, small = ([None] * layers for _ in range(5))
    output = None
    arrival = None
    for layer in reversed(range(layers)):
        (stream, normed, z, x_ext, bc_ext, conv_x, full_bc, step, cumul, raw, state_in, decay, mixed, pay, other) = saves[layer]
        final = layer == layers - 1
        operands = [grad, stream] if final else [grad, *arrival, saves[layer + 1][0], norm_gain]
        operands += [pay, other, z, mixed, full_bc, cumul, conv_x, gate_gain, weight_out]
        got = call(
            starred(gate_body, layer, final, inner),
            (
                shape_of((length, width), F32),
                shape_of((state, channels), BF16),
                shape_of((length, channels), F32),
                shape_of((length, channels), BF16),
                shape_of((length, channels), BF16),
                shape_of((length, width), BF16),
                shape_of((HALO, channels), F32),
                shape_of((HALO, heads), F32),
            ),
            operands,
            [VM] * (len(operands) - 1) + [layer_block(weight_out, layer)],
            name=f"gate{layer}",
        )
        first_out, d_state, d_mixed, d_z, gate_o, grad_b, gate_sum, d_skip = got
        if final:
            output = first_out
        else:
            grad = first_out
        later = entering(decay[0:1], d_state, True)
        d_x, d_bc, d_step, d_cumul = call(
            starred(pairs_body, layer),
            (
                shape_of((length, channels), F32),
                shape_of((length, 2 * state), F32),
                shape_of((length, heads), F32),
                shape_of((length, heads), F32),
            ),
            [d_mixed, conv_x, full_bc, step, cumul, state_in, skip_gain],
            scratch=[pltpu.VMEM((-(-heads // 8) * 8, length), F32)],
            name=f"pairs{layer}",
        )
        early[layer] = scattered(
            call(starred(early_body), shape_of((width, 2 * channels), BF16), [normed, d_z, grad_b, gate_o], name=f"early{layer}")
        )
        operands = [head, later, state_in, full_bc, conv_x, step, cumul, raw]
        operands += [log_rate, d_x, d_bc, d_step, d_cumul, d_z, x_ext, bc_ext, stream]
        operands += [taps_x, offset_x, taps_bc, offset_bc, bc_part]
        operands += [w_zx[layer], weight_bc, w_part[layer], w_step, gate_sum, d_skip]
        specs = [SM] + [VM] * 16
        specs += [layer_block(taps_x, layer), VM, layer_block(taps_bc, layer), VM, layer_block(bc_part, layer)]
        specs += [VM, layer_block(weight_bc, layer), VM, layer_block(w_step, layer), VM, VM]
        down, near, d_xin, d_own, d_part, d_raw, share[layer], small[layer] = call(
            starred(back_body, layer),
            (
                shape_of((length, width), BF16),
                shape_of((HALO, width), F32),
                shape_of((rows, channels), BF16),
                shape_of((rows, state), BF16),
                shape_of((rows, state), BF16),
                shape_of((length, heads), BF16),
                shape_of((HALO, width), F32),
                shape_of((HALO, channels), F32),
            ),
            operands,
            specs,
            [
                pltpu.VMEM((rows, channels), F32),
                pltpu.VMEM((rows, 2 * state), F32),
                pltpu.VMEM((rows + HALO, channels), F32),
                pltpu.VMEM((rows + HALO, 2 * state), F32),
            ],
            name=f"back{layer}",
        )
        arrival = (down, flip(down, "head", 1), to_next(near, -1, False), to_next(near, -1, True))
        late[layer] = scattered(
            call(starred(late_body), shape_of((width, channels + 128), BF16), [normed, d_xin, d_raw], name=f"late{layer}")
        )
        bc_grad[layer] = scattered(
            call(starred(bc_body), shape_of((width, state), BF16), [normed, d_own, flip(d_part, "head", 1)], name=f"bcw{layer}")
        )
    operands = [grad, *arrival, saves[0][0], norm_gain]
    grad = call(starred(final_body, 0), shape_of((length, width), F32), operands, name="final")

    mine, theirs = [], []
    for layer in range(layers):
        got = flip(share[layer], "head", 1)
        gains = share[layer][0:1] + got[0:1]
        shifted = jnp.concatenate([got[1 : 2 + kernel, state : 2 * state], jnp.zeros((1 + kernel, width - state), F32)], axis=1)
        mine.append(jnp.concatenate([gains, share[layer][1 : 2 + kernel] + shifted], axis=0))
    totals = [summed(jnp.concatenate([mine[layer], small[layer]], axis=0)) for layer in range(layers)]
    at = 2 + kernel

    def row(index, start=0, size=None):
        return jnp.stack([total[index, start : start + size] for total in totals])

    def table(index, size):
        return jnp.stack([total[index : index + kernel, :size] for total in totals])

    block = width // (lax.axis_size("batch") * lax.axis_size("seq"))
    return (
        output[None],
        grad[None],
        row(0, 0, width),
        jnp.stack([jnp.stack([e[:, :channels], l[:, :channels]], axis=1) for e, l in zip(early, late)]),
        jnp.stack(bc_grad),
        jnp.stack([l[:, channels : channels + heads] for l in late]),
        row(at + 2 + kernel, 0, heads),
        row(at + 2 + kernel, 128, heads),
        row(at + 2 + kernel, 256, heads),
        table(at + 1, channels),
        row(at + 1 + kernel, 0, channels),
        table(1, state),
        row(1 + kernel, 0, state),
        row(at, 0, channels),
        jnp.stack([e[:, channels:].T for e in early]),
    )


def solution(mesh):
    return jax.shard_map(
        body,
        mesh=mesh,
        in_specs=(
            P("batch", "seq", None),
            P("batch", "seq", None),
            P(),
            P(None, None, None, "head"),
            P(None, None, "head"),
            P(None, None, "head"),
            P(None, "head"),
            P(None, "head"),
            P(None, "head"),
            P(None, None, "head"),
            P(None, "head"),
            P(None, None, "head"),
            P(None, "head"),
            P(None, "head"),
            P(None, "head", None),
        ),
        out_specs=(
            P("batch", "seq", None),
            P("batch", "seq", None),
            P(),
            P(None, ("batch", "seq"), None, "head"),
            P(None, ("batch", "seq"), "head"),
            P(None, ("batch", "seq"), "head"),
            P(None, "head"),
            P(None, "head"),
            P(None, "head"),
            P(None, None, "head"),
            P(None, "head"),
            P(None, None, "head"),
            P(None, "head"),
            P(None, "head"),
            P(None, "head", ("batch", "seq")),
        ),
        check_vma=False,
    )
```
